128 devices in a mesh: aux: 32 (over x, z, y_hi), occ: 4 (over y_lo, core).
Axes of the slice: x: 4, y: 4 (y_hi: 2, y_lo: 2; y = y_hi * 2 + y_lo), z: 4, core: 2. Of those that a mesh axis runs over, the one named last changes fastest.
Arguments:
- factors: bfloat16 [3840, 8, 2560], P('aux', 'occ'), may hold values from -0.25 to 0.25
- pair_list: int32 [4, 2], replicated, may hold values from 0 to 3
- eps_occ: float32 [8], replicated, may hold values from -2 to -0.3
- eps_virt: float32 [2560], replicated, may hold values from 0.2 to 3
Outputs:
- energy_by_virtual: float32 [4, 4, 2560], P('occ', None, 'aux')
The draws below stay inside these ranges and needn't reach their ends.
All inputs are finite; a program needn't handle non-finite values.
Results may differ from the reference program's by a relative error of at most 0.0003.
Values may be sent and summed in bfloat16 or wider, within the bound.
No kernel may reach another device: no remote copies, remote signals or barrier semaphores. Data moves between devices by JAX's collectives and lax.ppermute only.
A program may use at most 128 MiB of HBM per device.

```python
import jax
import jax.numpy as jnp
from jax import lax

NAUX = 3840
W = 2560
ORB_DEV = 2
NORB = 8
NPAIR = 4
N_OCC = 4


def plant(entries, rng, least, largest):
    dims = entries.shape
    index_at = [jax.random.randint(jax.random.fold_in(rng, axis), (), 0, dims[axis]) for axis in range(len(dims))]
    entries = entries.at[tuple(index_at)].set(least)
    longest = dims.index(max(dims))
    index_at[longest] = (index_at[longest] + 1) % dims[longest]
    return entries.at[tuple(index_at)].set(largest)


def block_levels(own_key, shape, shards, low, high):
    factor_of = 1.0
    for position, blocks in shards:
        draws = jax.random.uniform(jax.random.fold_in(jax.random.fold_in(own_key, 6), position), (blocks,), jnp.float32, low / len(shards), high / len(shards))
        factor_of = factor_of * jnp.repeat(jnp.exp(draws), shape[position] // blocks).reshape((-1,) + (1,) * (len(shape) - 1 - position))
    return factor_of


def gaussian(stream_key, dims, scale, most, shards=(), kind=jnp.bfloat16):
    gain = block_levels(stream_key, dims, shards, -0.22, 0.18) if shards else 1.0
    values = jax.random.normal(stream_key, dims, jnp.float32) * scale * gain
    return jnp.minimum(jnp.maximum(values, -most), most).astype(kind)


def setup_inputs(seed: int = 0) -> dict:
    seeds = jax.random.split(jax.random.key(seed), 5)
    return {
        "factors": gaussian(seeds[0], (NAUX, NORB, W), ((W * NAUX) ** -0.25), 0.25, ((0, 32), (1, 4))),
        "pair_list": plant(jax.random.randint(seeds[1], (NPAIR, 2), 0, N_OCC), jax.random.fold_in(seeds[1], 1), 0, N_OCC - 1).astype(jnp.int32),
        "eps_occ": jnp.clip(jax.random.uniform(seeds[2], (NORB,), jnp.float32, -2.0, -0.3), -2.0, -0.3),
        "eps_virt": jnp.clip(jax.random.uniform(seeds[3], (W,), jnp.float32, 0.2, 3.0), 0.2, 3.0),
    }


def reference(factors, pair_list, eps_occ, eps_virt):
    def block_energy(pair_row):
        def orbital_pair(flat):
            left_index = (pair_row[0] * ORB_DEV + flat // ORB_DEV).astype(jnp.int32)
            right_index = (pair_row[1] * ORB_DEV + flat % ORB_DEV).astype(jnp.int32)
            left_orb = lax.dynamic_index_in_dim(factors, left_index, 1, keepdims=False)
            right_orb = lax.dynamic_index_in_dim(factors, right_index, 1, keepdims=False)
            coulomb = jnp.dot(left_orb.T, right_orb, preferred_element_type=jnp.float32)
            denominator = eps_virt[:, None] + eps_virt[None, :] - eps_occ[left_index] - eps_occ[right_index]
            return -jnp.sum(coulomb * (2.0 * coulomb - coulomb.T) / denominator, axis=1)

        return lax.map(orbital_pair, jnp.arange(ORB_DEV * ORB_DEV, dtype=jnp.int32))

    return lax.map(block_energy, pair_list)
```

```python
import functools

import jax
import jax.numpy as jnp
from jax import lax
from jax.experimental import pallas as pl
from jax.experimental.pallas import tpu as pltpu
from jax.sharding import Mesh, PartitionSpec as P

AXES = ("x", "z", "yh", "yl", "c")
SIZES = {"x": 4, "z": 4, "y": 4, "c": 2}


def flat_id(x, z, y, c):
    return (((x * 4 + z) * 2 + y // 2) * 2 + y % 2) * 2 + c


def shift_pairs(axis, shift):
    pairs = []
    for x in range(4):
        for z in range(4):
            for y in range(4):
                for c in range(2):
                    at = {"x": x, "z": z, "y": y, "c": c}
                    to = dict(at)
                    to[axis] = (at[axis] + shift) % SIZES[axis]
                    pairs.append((flat_id(**at), flat_id(**to)))
    return pairs


def send(value, axis, shift):
    return lax.ppermute(value, AXES, shift_pairs(axis, shift))


def ring_gather(own, axis, halves):
    low, high = halves
    below = send(own, axis, 1)
    above = send(own, axis, -1)
    far_low = send(below[:, :low], axis, 1)
    far_high = send(above[:, low:], axis, -1)
    return own, above, below, far_low, far_high


def pair_kernel(n_ops, half, eo_ref, eb_ref, ea_ref, *rest):
    arrays = rest[: 4 * n_ops]
    out_ref = rest[4 * n_ops]
    a_buf, b_buf, a_sib, b_sib, acc, sems = rest[4 * n_ops + 1:]
    a_mine, a_other, b_mine, b_other = (
        arrays[k * n_ops:(k + 1) * n_ops] for k in range(4)
    )
    step = pl.program_id(0)

    def pick(pieces, outer, inner, slot, buf, sem, which):
        own, above, below, far_low, far_high = pieces

        def go(ref, first):
            src = ref.at[which, inner - first] if which == 0 else ref.at[:, inner - first]
            pltpu.make_async_copy(src, buf.at[slot], sem).start()

        pl.when(outer == 0)(lambda: go(own, 0))
        pl.when(outer == 1)(lambda: go(above, 0))
        pl.when(outer == 3)(lambda: go(below, 0))
        pl.when(jnp.logical_and(outer == 2, inner < half))(lambda: go(far_low, 0))
        pl.when(jnp.logical_and(outer == 2, inner >= half))(lambda: go(far_high, half))

    def fetch(at, slot):
        dz, dx = at // 4, at % 4
        pick(a_mine, dz, dx, slot, a_buf, sems.at[slot, 0], None)
        pick(b_mine, dx, dz, slot, b_buf, sems.at[slot, 1], None)
        pick(a_other, dz, dx, slot, a_sib, sems.at[slot, 2], 0)
        pick(b_other, dx, dz, slot, b_sib, sems.at[slot, 3], 0)

    @pl.when(step == 0)
    def _():
        fetch(step, 0)

    slot = lax.rem(step, 2)

    @pl.when(step + 1 < pl.num_programs(0))
    def _():
        fetch(step + 1, lax.rem(step + 1, 2))

    pltpu.make_async_copy(a_mine[0].at[:, 0], a_buf.at[slot], sems.at[slot, 0]).wait()
    pltpu.make_async_copy(b_mine[0].at[:, 0], b_buf.at[slot], sems.at[slot, 1]).wait()
    pltpu.make_async_copy(a_other[0].at[0, 0], a_sib.at[slot], sems.at[slot, 2]).wait()
    pltpu.make_async_copy(b_other[0].at[0, 0], b_sib.at[slot], sems.at[slot, 3]).wait()

    def dot(left, right):
        return lax.dot_general(
            left, right, (((0,), (0,)), ((), ())), preferred_element_type=jnp.float32
        )

    a_i = (a_buf[slot, 0], a_sib[slot])
    b_i = (b_buf[slot, 0], b_sib[slot])
    a_j, b_j = a_buf[slot, 1], b_buf[slot, 1]

    @pl.when(step == 0)
    def _():
        acc[...] = jnp.zeros_like(acc)

    for u in range(2):
        acc[0, u] += dot(b_j, a_i[u])
        acc[1, u] += dot(b_i[u], a_j)

    @pl.when(step == pl.num_programs(0) - 1)
    def _():
        for u in range(2):
            direct, swapped = acc[0, u], acc[1, u]
            denominator = ea_ref[...] + eb_ref[...] - eo_ref[0, u] - eo_ref[0, 2]
            term = direct * (2.0 * direct - swapped) / denominator
            out_ref[pl.ds(u, 1), :] = -jnp.sum(term, axis=0, keepdims=True)


def pair_energies(a_mine, a_other, b_mine, b_other, occ_levels, ea, eb, half):
    _, _, rows, span = a_mine[0].shape
    n_ops = len(a_mine)
    any_spec = pl.BlockSpec(memory_space=pl.ANY)
    return pl.pallas_call(
        functools.partial(pair_kernel, n_ops, half),
        out_shape=jax.ShapeDtypeStruct((2, span), jnp.float32),
        grid=(16,),
        in_specs=[
            pl.BlockSpec(memory_space=pltpu.SMEM),
            pl.BlockSpec((span, 1), lambda t: (0, 0)),
            pl.BlockSpec((1, span), lambda t: (0, 0)),
        ] + [any_spec] * (4 * n_ops),
        out_specs=pl.BlockSpec((2, span), lambda t: (0, 0)),
        scratch_shapes=[
            pltpu.VMEM((2, 2, rows, span), jnp.bfloat16),
            pltpu.VMEM((2, 2, rows, span), jnp.bfloat16),
            pltpu.VMEM((2, rows, span), jnp.bfloat16),
            pltpu.VMEM((2, rows, span), jnp.bfloat16),
            pltpu.VMEM((2, 2, span, span), jnp.float32),
            pltpu.SemaphoreType.DMA((2, 4)),
        ],
        compiler_params=pltpu.CompilerParams(
            dimension_semantics=("arbitrary",), vmem_limit_bytes=48 * 1024 * 1024
        ),
    )(occ_levels, eb, ea, *a_mine, *a_other, *b_mine, *b_other)


def on_device(factors, pair_list, eps_occ, eps_virt):
    local_q, orb_local, virt_width = factors.shape
    span = virt_width // 4
    x, z, yh, yl, c = (lax.axis_index(name) for name in AXES)
    y = yh * 2 + yl
    pair = pair_list[yl * 2 + yh]

    by_orb = factors.transpose(1, 0, 2)
    keep = lax.dynamic_index_in_dim(by_orb, c, 0, keepdims=True)
    away = lax.dynamic_index_in_dim(by_orb, 1 - c, 0, keepdims=True)
    held = jnp.concatenate([keep, send(away, "c", 1)], axis=0)

    below = send(held, "y", 1)
    above = send(held, "y", -1)
    far_low = send(below[:1], "y", 1)
    far_high = send(above[1:], "y", -1)
    candidates = jnp.concatenate([held, above, far_low, far_high, below], axis=0)

    def block_of(which):
        parts = []
        for half in range(2):
            offset = (half * 2 + pair[which] // 2 - y) % 4
            parts.append(
                lax.dynamic_index_in_dim(
                    candidates, offset * 2 + ((pair[which] % 2) ^ c), 0, keepdims=False
                )
            )
        return jnp.concatenate(parts, axis=0)

    picked = jnp.stack([block_of(0), block_of(1)], axis=0)

    def columns(of):
        return lax.dynamic_slice_in_dim(picked, (of % 4) * span, span, 2)

    def exchange(me, axis):
        pieces = [columns(me)]
        got = {d: send(columns(me + d), axis, d) for d in (1, 2, 3)}
        pieces += [got[3], got[2], got[1]]
        return jnp.stack(pieces, axis=1)

    rows_own = exchange(x, "x")
    cols_own = exchange(z, "z")
    a_mine = ring_gather(rows_own, "z", (2, 2))
    b_mine = ring_gather(cols_own, "x", (2, 2))
    a_other = [send(v, "c", 1) for v in a_mine]
    b_other = [send(v, "c", 1) for v in b_mine]

    left = lax.dynamic_slice_in_dim(eps_occ, pair[0] * orb_local, orb_local)
    right = lax.dynamic_slice_in_dim(eps_occ, pair[1] * orb_local, orb_local)
    levels = jnp.stack([left[c], left[1 - c], right[c]]).reshape(1, 3)
    ea = lax.dynamic_slice_in_dim(eps_virt, x * span, span).reshape(1, span)
    eb = lax.dynamic_slice_in_dim(eps_virt, z * span, span).reshape(span, 1)
    energies = pair_energies(a_mine, a_other, b_mine, b_other, levels, ea, eb, 2)

    energies = jnp.where(c == 0, energies, energies[::-1])
    sub = span // 8
    parts = energies.reshape(2, 8, sub).transpose(1, 0, 2)
    parts = jnp.broadcast_to(parts.reshape(8, 1, 2, sub), (8, 2, 2, sub)).reshape(16, 2, sub)
    got = lax.all_to_all(parts, ("z", "yh", "c"), split_axis=0, concat_axis=0, tiled=True)
    got = got.reshape(4, 2, 2, 2, sub)
    got = lax.dynamic_index_in_dim(got, c, 1, keepdims=False)
    total = jnp.sum(got, axis=0).transpose(1, 0, 2)
    return total.reshape(1, 4, sub)


def solution(mesh):
    torus = Mesh(mesh.devices.reshape(4, 4, 2, 2, 2), AXES)
    return jax.shard_map(
        on_device,
        mesh=torus,
        in_specs=(P(("x", "z", "yh"), ("yl", "c"), None), P(), P(), P()),
        out_specs=P(("yl", "c"), None, ("x", "z", "yh")),
        check_vma=False,
    )
```
